512 devices in a mesh: dp: 64 (over z, x, core), group: 8 (over y).
Axes of the slice: x: 4, y: 8, z: 8, core: 2. Of those that a mesh axis runs over, the one named last changes fastest.
Arguments:
- queries: bfloat16 [8192, 2, 2048], P('dp', None, 'group'), may hold values from -21 to 21
- new_keys: bfloat16 [8192, 2048], P('dp', 'group'), may hold values from -12 to 12
- new_values: bfloat16 [8192, 2048], P('dp', 'group'), may hold values from -6 to 6
- cache_keys: bfloat16 [64, 2048, 2048], P('dp', None, 'group'), may hold values from -6 to 6
- cache_values: bfloat16 [64, 2048, 2048], P('dp', None, 'group'), may hold values from -6 to 6
- lengths: int32 [64], P('dp'), may hold values from 1 to 2048, as said below
- att_gates: float32 [8192, 2], P('dp'), may hold values from 0.1 to 0.9
- resid: bfloat16 [8192, 2048], P('dp', 'group'), may hold values from -72 to 72
- norm_gain: float32 [2048], P('group'), may hold values from 0.5 to 1.5
- expert_ids: int32 [8192, 2], P('dp'), may hold values from 0 to 7, all different within a row; in each aligned block of 128 rows (0 to 127, 128 to 255, ...) at most 40 rows name the same one
- expert_gates: float32 [8192, 2], P('dp'), may hold values from 0.1 to 0.9
- w_gate: bfloat16 [64, 2048, 704], P('dp', 'group'), may hold values from -0.125 to 0.125
- w_up: bfloat16 [64, 2048, 704], P('dp', 'group'), may hold values from -0.125 to 0.125
- w_down: bfloat16 [64, 704, 2048], P('dp', None, 'group'), may hold values from -0.078125 to 0.078125
Outputs:
- attended: bfloat16 [8192, 2048], P('dp', 'group')
- mixed: bfloat16 [8192, 2048], P('dp', 'group')
The draws below stay inside these ranges and needn't reach their ends.
Inputs may be any that keep to these rules, and one draw needn't show every extreme that they name: `expert_ids`: in the tokens of one request (aligned blocks of 128 rows) no expert is named more than 40 times, a bound that some block reaches; the two experts of a row differ. `lengths`: some request has exactly 2048 cached tokens.
All inputs are finite; a program needn't handle non-finite values.
Results may differ from the reference program's by a relative error of at most 0.0055.
Values may be sent and summed in bfloat16 or wider, within the bound.
No kernel may reach another device: no remote copies, remote signals or barrier semaphores. Data moves between devices by JAX's collectives and lax.ppermute only.
A program may use at most 64 MiB of HBM per device.

```python
import math
import jax
import jax.numpy as jnp
import numpy as np
from jax import lax

D = 2048
KV_HEADS = 16
HD = 128
EXPERTS = 8
FF = 5632
TOK_DEV = 128
CACHE = 2048
CAP = 40
OWNERS = 8
FFB = 704
REQUESTS = 64
TOKENS = 8192
N_DP = 64


def query_key_pair(key):
    query_seed = jax.random.fold_in(key, 11)
    keys_seed = jax.random.fold_in(key, 12)
    base_query = jnp.clip(jax.random.normal(query_seed, (TOKENS, 2, KV_HEADS * HD), jnp.float32), -3.0, 3.0)
    base_keys = jnp.clip(jax.random.normal(keys_seed, (TOKENS, KV_HEADS * HD), jnp.float32), -3.0, 3.0)
    query_out = 2.5 * base_query
    keys_out = base_keys
    return (query_out, keys_out)


def draw_queries(key, part):
    return query_key_pair(key)[0].astype(jnp.bfloat16)


def draw_new_keys(key, part):
    return query_key_pair(key)[1].astype(jnp.bfloat16)


def draw_lengths(key, part):
    drawn = jax.random.randint(jax.random.fold_in(key, 21), (REQUESTS,), 1, CACHE + 1)
    chosen = jax.random.randint(jax.random.fold_in(key, 22), (), 0, REQUESTS)
    return jnp.where(jnp.arange(REQUESTS) == chosen, CACHE, drawn).astype(jnp.int32)


def draw_resid(key, part):
    base = jnp.clip(jax.random.normal(jax.random.fold_in(key, 31), (TOKENS, D), jnp.float32), -6.0, 6.0)
    column = jnp.sqrt(1.0 + 2.0 * jnp.arange(D, dtype=jnp.float32) / (D - 1))
    values = base * column[None, :]
    return values.astype(jnp.bfloat16)


def steps_of(stream_key, dims, cuts, low, high):
    loudness, own = 1.0, jax.random.fold_in(stream_key, 6)
    for dim, blocks in cuts:
        draws = jnp.exp(jax.random.uniform(jax.random.fold_in(own, dim), (blocks,), jnp.float32, low / len(cuts), high / len(cuts)))
        loudness = loudness * jnp.repeat(draws, dims[dim] // blocks).reshape([-1 if axis == dim else 1 for axis in range(len(dims))])
    return loudness


def shared_out(stream_key, own, number, rows, count, top, bound, lean):
    order = jax.random.permutation(stream_key, count)
    heavy_load, usual = shares(count, rows * top, bound, lean, True), shares(count, rows * top, bound, lean, False)
    places = jnp.arange(count)

    def named(sizes, offset_by):
        used = int((sizes > 0).sum())
        fixed = max(1, used // 4)
        shifted = fixed + (places - fixed + offset_by * (used - fixed)) % max(1, count - fixed)
        return jnp.zeros((count,), jnp.int32).at[order[jnp.where(places < fixed, places, shifted)]].set(jnp.asarray(sizes, jnp.int32))

    sizes = jnp.where(number % 4 == 0, named(heavy_load, number // 4), named(usual, number - number // 4 - 1))
    mixed = jax.random.permutation(jax.random.fold_in(own, 3), count)
    source_of, taker = mixed[0:count // 2 * 2:2], mixed[1:count // 2 * 2:2]
    slack = jnp.minimum(sizes[source_of] - 1, bound - sizes[taker]) // 2
    slack = jnp.where((source_of == order[0]) | (taker == order[0]) | (sizes[taker] == 0), 0, jnp.maximum(slack, 0))
    shifted = jax.random.randint(jax.random.fold_in(own, 4), (count // 2,), 0, 1 << 20) % (slack + 1)
    sizes = sizes.at[source_of].add(-shifted).at[taker].add(shifted)
    labels = jnp.searchsorted(jnp.cumsum(sizes), jnp.arange(rows * top), side="right").astype(jnp.int32)
    grid = labels.reshape(top, rows).T
    grid = grid[jax.random.permutation(jax.random.fold_in(own, 1), rows)]
    offset_by = jax.random.randint(jax.random.fold_in(own, 2), (rows, 1), 0, top)
    return jnp.take_along_axis(grid, (jnp.arange(top)[None, :] + offset_by) % top, axis=1)


def shares(count, total, bound, lean, full):
    portions = [(1 << 20) // math.isqrt(standing ** lean) + 1 for standing in range(1, count + 1)]
    largest = bound if full else min(bound, max(-(-total // count), total * portions[0] // sum(portions)))
    least = 1 if total - largest >= count - 1 else 0
    given, rest = [largest] + [least] * (count - 1), total - largest - least * (count - 1)
    while rest > 0:
        free = [i for i in range(1, count) if given[i] < largest] or [i for i in range(1, count) if given[i] < bound]
        mass, left = sum([portions[i] for i in free]), rest
        for i in free:
            addition = min(bound - given[i], max(1, left * portions[i] // mass), rest)
            given[i] = given[i] + addition
            rest = rest - addition
    return np.array(given)


def noise(stream_key, extent, scale, bound, pieces=(), kind=jnp.bfloat16):
    values = scale * jax.random.normal(stream_key, extent, jnp.float32)
    if pieces:
        values = values * steps_of(stream_key, extent, pieces, -0.22, 0.18)
    return jnp.clip(values, -bound, bound).astype(kind)


def setup_inputs(seed: int = 0) -> dict:
    key_of = jax.random.split(jax.random.key(seed), 15)
    queries = draw_queries(jax.random.fold_in(key_of[14], 71), 0)
    new_keys = draw_new_keys(jax.random.fold_in(key_of[14], 71), 0)
    new_values = noise(key_of[2], (TOKENS, KV_HEADS * HD), 1.0, 6.0, ((0, 64), (1, 8)))
    cache_keys = noise(key_of[3], (REQUESTS, CACHE, KV_HEADS * HD), 1.0, 6.0, ((0, 64), (2, 8)))
    cache_values = noise(key_of[4], (REQUESTS, CACHE, KV_HEADS * HD), 1.0, 6.0, ((0, 64), (2, 8)))
    lengths = draw_lengths(jax.random.fold_in(key_of[14], 71), 0)
    att_gates = jnp.clip(0.1 + 0.79999997 * jax.random.uniform(key_of[6], (TOKENS, 2), jnp.float32) ** steps_of(key_of[6], (TOKENS, 2), ((0, 64),), -0.2, 0.2), 0.1, 0.9)
    resid = draw_resid(jax.random.fold_in(key_of[14], 71), 0)
    norm_gain = jnp.clip(1.0 + 0.1 * jax.random.normal(key_of[8], (D,), jnp.float32), 0.5, 1.5)
    expert_ids_keys = jax.random.split(jax.random.fold_in(key_of[9], 1), TOKENS // TOK_DEV)
    expert_ids_turns = jax.random.permutation(jax.random.fold_in(key_of[9], 3), TOKENS // TOK_DEV)
    expert_ids = jax.vmap(lambda own, number: shared_out(jax.random.fold_in(key_of[9], 2), own, number, TOK_DEV, EXPERTS, 2, CAP, 2))(expert_ids_keys, expert_ids_turns).reshape((TOKENS, 2))
    expert_gates = jnp.clip(0.1 + 0.79999997 * jax.random.uniform(key_of[10], (TOKENS, 2), jnp.float32) ** steps_of(key_of[10], (TOKENS, 2), ((0, 64),), -0.2, 0.2), 0.1, 0.9)
    w_gate = noise(key_of[11], (EXPERTS * OWNERS, D, FFB), D ** -0.5, 0.125, ((0, 64), (1, 8)))
    w_up = noise(key_of[12], (EXPERTS * OWNERS, D, FFB), D ** -0.5, 0.125, ((0, 64), (1, 8)))
    w_down = noise(key_of[13], (EXPERTS * OWNERS, FFB, D), FF ** -0.5, 0.078125, ((0, 64), (2, 8)))
    return dict(queries=queries, new_keys=new_keys, new_values=new_values, cache_keys=cache_keys, cache_values=cache_values, lengths=lengths, att_gates=att_gates, resid=resid, norm_gain=norm_gain, expert_ids=expert_ids, expert_gates=expert_gates, w_gate=w_gate, w_up=w_up, w_down=w_down)


def pair_slots(expert_rows):
    flat_ids = expert_rows.reshape(-1)
    onehot = (flat_ids[:, None] == jnp.arange(EXPERTS, dtype=jnp.int32)[None, :]).astype(jnp.int32)
    running = jnp.cumsum(onehot, axis=0)
    return (lax.optimization_barrier(jnp.sum(running * onehot, axis=1)) - 1).astype(jnp.int32).reshape(expert_rows.shape)

def attend_request(request_args):
    query_rows, key_new, value_new, key_cache, value_cache, length, gate_rows = request_args
    row_count = query_rows.shape[0]
    query_h = query_rows.reshape(row_count, 2, KV_HEADS, HD).astype(jnp.float32)
    keys_c = key_cache.reshape(CACHE, KV_HEADS, HD).astype(jnp.float32)
    keys_n = key_new.reshape(row_count, KV_HEADS, HD).astype(jnp.float32)
    values_c = value_cache.reshape(CACHE, KV_HEADS, HD).astype(jnp.float32)
    values_n = value_new.reshape(row_count, KV_HEADS, HD).astype(jnp.float32)
    score_scale = HD ** (-0.5)
    high = lax.Precision.HIGHEST
    scores_c = jnp.einsum('tshd,khd->shtk', query_h, keys_c, precision=high) * score_scale
    scores_n = jnp.einsum('tshd,khd->shtk', query_h, keys_n, precision=high) * score_scale
    live_keys = jnp.arange(CACHE, dtype=jnp.int32) < length
    scores_c = jnp.where(live_keys[None, None, None, :], scores_c, -jnp.inf)
    position = jnp.arange(row_count, dtype=jnp.int32)
    causal = position[None, :] <= position[:, None]
    scores_n = jnp.where(causal[None, None], scores_n, -jnp.inf)
    row_max = jnp.maximum(lax.optimization_barrier(jnp.max(scores_c, axis=-1)), lax.optimization_barrier(jnp.max(scores_n, axis=-1)))
    exp_c = jnp.exp(scores_c - row_max[..., None])
    exp_n = jnp.exp(scores_n - row_max[..., None])
    row_total = lax.optimization_barrier(jnp.sum(exp_c, axis=-1)) + lax.optimization_barrier(jnp.sum(exp_n, axis=-1))
    probs_c = lax.optimization_barrier((exp_c / row_total[..., None]).astype(jnp.bfloat16)).astype(jnp.float32)
    probs_n = lax.optimization_barrier((exp_n / row_total[..., None]).astype(jnp.bfloat16)).astype(jnp.float32)
    output = jnp.einsum('shtk,khd->tshd', probs_c, values_c, precision=high)
    output = output + jnp.einsum('shtk,khd->tshd', probs_n, values_n, precision=high)
    output = output.reshape(row_count, 2, KV_HEADS * HD)
    return lax.optimization_barrier(jnp.sum(output * gate_rows[:, :, None], axis=1))

def reference(queries, new_keys, new_values, cache_keys, cache_values, lengths, att_gates, resid, norm_gain, expert_ids, expert_gates, w_gate, w_up, w_down):
    requests = N_DP
    attention = lax.map(attend_request, (queries.reshape(requests, TOK_DEV, 2, KV_HEADS * HD), new_keys.reshape(requests, TOK_DEV, KV_HEADS * HD), new_values.reshape(requests, TOK_DEV, KV_HEADS * HD), cache_keys, cache_values, lengths, att_gates.reshape(requests, TOK_DEV, 2)))
    attention = attention.reshape(TOKENS, D)
    attended = attention.astype(jnp.bfloat16)
    mixed_in = resid.astype(jnp.float32) + attention
    squares = lax.optimization_barrier(jnp.sum(mixed_in * mixed_in, axis=1, keepdims=True))
    normed = (mixed_in / jnp.sqrt(squares / D + 1e-05) * norm_gain[None, :]).astype(jnp.bfloat16)
    id_blocks = expert_ids.reshape(requests, TOK_DEV, 2)
    slot_index = jax.vmap(pair_slots)(id_blocks)
    buffer_rows = (jnp.arange(requests, dtype=jnp.int32)[:, None, None] * CAP + slot_index).reshape(-1)
    expert_flat = id_blocks.reshape(-1)
    pair_rows = jnp.repeat(normed, 2, axis=0)
    buffers = jnp.zeros((EXPERTS, requests * CAP, D), jnp.bfloat16).at[expert_flat, buffer_rows].set(pair_rows)
    owners = requests // EXPERTS
    gate_w = w_gate.reshape(EXPERTS, owners, D, FF // owners)
    up_w = w_up.reshape(EXPERTS, owners, D, FF // owners)
    down_w = w_down.reshape(EXPERTS, owners, FF // owners, D)

    def expert_out(expert_args):
        features, gate_e, up_e, down_e = expert_args

        def owner_step(carry, owner_args):
            gate_o, up_o, down_o = owner_args
            gate_act = jnp.dot(features, gate_o, preferred_element_type=jnp.float32)
            up_act = jnp.dot(features, up_o, preferred_element_type=jnp.float32)
            hidden = (jax.nn.silu(gate_act) * up_act).astype(jnp.bfloat16)
            part = lax.optimization_barrier(jnp.dot(hidden, down_o, preferred_element_type=jnp.float32).astype(jnp.bfloat16))
            return (carry + part.astype(jnp.float32), None)
        start = jnp.zeros((features.shape[0], D), jnp.float32)
        summed, unused = lax.scan(owner_step, start, (gate_e, up_e, down_e))
        return summed
    outputs = lax.map(expert_out, (buffers, gate_w, up_w, down_w))
    picked = outputs[expert_flat, buffer_rows].reshape(TOKENS, 2, D)
    expert_mix = lax.optimization_barrier(jnp.sum(picked * expert_gates[:, :, None], axis=1))
    mixed = (mixed_in + expert_mix).astype(jnp.bfloat16)
    return (attended, mixed)
```

```python
import jax
import jax.numpy as jnp
from jax import lax
from jax.experimental import pallas as pl
from jax.experimental.pallas import tpu as pltpu
from jax.sharding import Mesh, PartitionSpec as P

D = 2048
HD = 128
EXPERTS = 8
CACHE = 2048
CAP = 40
TOK = 128
FEAT = 256
FFB = 704
GROUPS = 8
PER = CAP // GROUPS
MAIN = 640
TAIL = FFB - MAIN
WIDE = 2 * FFB
SLOTS_W = PER * FEAT
SEND_W = SLOTS_W + 128
ROWS = 64
TROWS = PER * ROWS
VMEM = 56 * 1024 * 1024

f32 = jnp.float32
bf16 = jnp.bfloat16


def params():
    return pltpu.CompilerParams(vmem_limit_bytes=VMEM)


def pack_kernel(gate_ref, up_ref, down_ref, out_ref):
    out_ref[0:FEAT, 0:MAIN] = gate_ref[0, :, 0:MAIN]
    out_ref[0:FEAT, MAIN : 2 * MAIN] = up_ref[0, :, 0:MAIN]
    out_ref[0:FEAT, 2 * MAIN : WIDE] = jnp.concatenate(
        [gate_ref[0, :, MAIN:FFB], up_ref[0, :, MAIN:FFB]], axis=1
    )
    for q in range(MAIN // 128):
        out_ref[FEAT : FEAT + 128, q * 256 : (q + 1) * 256] = down_ref[0, q * 128 : (q + 1) * 128, :]
    out_ref[FEAT : FEAT + TAIL, 2 * MAIN : WIDE] = down_ref[0, MAIN:FFB, 0:128]
    out_ref[FEAT + TAIL : FEAT + 128, 2 * MAIN : WIDE] = down_ref[0, MAIN:FFB, 128:256]


def pack_weights(w_gate, w_up, w_down):
    return pl.pallas_call(
        pack_kernel,
        out_shape=jax.ShapeDtypeStruct((FEAT + 128, WIDE), bf16),
        compiler_params=params(),
        name="pack_weights",
    )(w_gate, w_up, w_down)


def slot_dests(ids):
    lane = lax.broadcasted_iota(jnp.int32, (TOK, 128), 1)
    row = lax.broadcasted_iota(jnp.int32, (TOK, 128), 0)
    first = ids[:, 0:1] == lane
    second = ids[:, 1:2] == lane
    named = jnp.where(first | second, 1.0, 0.0).astype(bf16)
    earlier = jnp.where(lane < row, 1.0, 0.0).astype(bf16)
    count = jnp.dot(earlier, named, preferred_element_type=f32)
    dest = []
    for k, hit in ((0, first), (1, second)):
        slot = jnp.sum(jnp.where(hit, count, 0.0), axis=1, keepdims=True).astype(jnp.int32)
        dest.append(ids[:, k : k + 1] * CAP + slot)
    return dest


def slot_values(i):
    lane = lax.broadcasted_iota(jnp.int32, (TOK, ROWS), 1)
    return (lane & 7) * CAP + (lane >> 3) * PER + i


def attend_kernel(
    len_ref, q_ref, kn_ref, vn_ref, kc_ref, vc_ref, ag_ref, res_ref, gain_ref, ids_ref,
    att_ref, mix_ref, send_ref,
):
    length = len_ref[0]
    neg = -1e30
    scale = HD ** (-0.5)
    live = lax.broadcasted_iota(jnp.int32, (TOK, CACHE), 1) < length
    causal = lax.broadcasted_iota(jnp.int32, (TOK, TOK), 1) <= lax.broadcasted_iota(jnp.int32, (TOK, TOK), 0)
    gates = ag_ref[...]
    nt = (((1,), (1,)), ((), ()))
    heads = []
    for h in range(FEAT // HD):
        cols = slice(h * HD, (h + 1) * HD)
        key_c, val_c = kc_ref[0, :, cols], vc_ref[0, :, cols]
        key_n, val_n = kn_ref[:, cols], vn_ref[:, cols]
        mixed_head = jnp.zeros((TOK, HD), f32)
        for s in range(2):
            q = q_ref[:, s * FEAT + h * HD : s * FEAT + (h + 1) * HD]
            sc = lax.dot_general(q, key_c, nt, preferred_element_type=f32) * scale
            sc = jnp.where(live, sc, neg)
            sn = lax.dot_general(q, key_n, nt, preferred_element_type=f32) * scale
            sn = jnp.where(causal, sn, neg)
            top = jnp.maximum(jnp.max(sc, axis=1, keepdims=True), jnp.max(sn, axis=1, keepdims=True))
            pc = jnp.exp(sc - top)
            pn = jnp.exp(sn - top)
            inv = 1.0 / (jnp.sum(pc, axis=1, keepdims=True) + jnp.sum(pn, axis=1, keepdims=True))
            out = jnp.dot((pc * inv).astype(bf16), val_c, preferred_element_type=f32)
            out = out + jnp.dot((pn * inv).astype(bf16), val_n, preferred_element_type=f32)
            mixed_head = mixed_head + gates[:, s : s + 1] * out
        heads.append(mixed_head)
    attention = jnp.concatenate(heads, axis=1)
    att_ref[...] = attention.astype(bf16)
    mixed_in = res_ref[...].astype(f32) + attention
    mix_ref[...] = mixed_in
    scaled = (mixed_in * gain_ref[...]).astype(bf16)
    square = jnp.sum(mixed_in * mixed_in, axis=1, keepdims=True)
    high = square.astype(bf16).astype(f32)
    mid = (square - high).astype(bf16).astype(f32)
    low = square - high - mid
    dest = slot_dests(ids_ref[...])
    tn = (((0,), (0,)), ((), ()))
    lane = lax.broadcasted_iota(jnp.int32, (TOK, 128), 1)
    squares = jnp.zeros((ROWS, 128), f32)
    for i in range(PER):
        value = slot_values(i)
        pick = jnp.where((dest[0] == value) | (dest[1] == value), 1.0, 0.0).astype(bf16)
        block = lax.dot_general(pick, scaled, tn, preferred_element_type=f32)
        send_ref[:, i * FEAT : (i + 1) * FEAT] = block.astype(bf16)
        parts = jnp.where(lane == 3 * i, high, jnp.where(lane == 3 * i + 1, mid, jnp.where(lane == 3 * i + 2, low, 0.0)))
        squares = squares + lax.dot_general(pick, parts.astype(bf16), tn, preferred_element_type=f32)
    send_ref[:, SLOTS_W:SEND_W] = squares.astype(bf16)


def attend(length, q, kn, vn, kc, vc, ag, res, gain, ids):
    vm = pl.BlockSpec(memory_space=pltpu.VMEM)
    return pl.pallas_call(
        attend_kernel,
        in_specs=[pl.BlockSpec(memory_space=pltpu.SMEM)] + [vm] * 9,
        out_specs=[vm] * 3,
        out_shape=[
            jax.ShapeDtypeStruct((TOK, FEAT), bf16),
            jax.ShapeDtypeStruct((TOK, FEAT), f32),
            jax.ShapeDtypeStruct((ROWS, SEND_W), bf16),
        ],
        compiler_params=params(),
        name="attend",
    )(length, q, kn, vn, kc, vc, ag, res, gain, ids)


def arrange_kernel(got_ref, x_ref, inv_ref):
    total = jnp.zeros((8, 8, 128), f32)
    for f in range(8):
        rows = slice(f * 8, (f + 1) * 8)
        for i in range(PER):
            piece = got_ref[:, rows, i * FEAT : (i + 1) * FEAT].astype(f32).reshape(ROWS, FEAT)
            x_ref[f, i * ROWS : (i + 1) * ROWS, :] = piece.astype(bf16)
        total = total + got_ref[:, rows, SLOTS_W:SEND_W].astype(f32)
    total = total.reshape(ROWS, 128)
    lane = lax.broadcasted_iota(jnp.int32, (ROWS, 128), 1)
    for i in range(PER):
        mine = (lane >= 3 * i) & (lane < 3 * i + 3)
        square = jnp.sum(jnp.where(mine, total, 0.0), axis=1, keepdims=True)
        inv_ref[i * ROWS : (i + 1) * ROWS, :] = jnp.broadcast_to(1.0 / jnp.sqrt(square / D + 1e-05), (ROWS, 128))


def arrange(got):
    return pl.pallas_call(
        arrange_kernel,
        out_shape=[
            jax.ShapeDtypeStruct((8, TROWS, FEAT), bf16),
            jax.ShapeDtypeStruct((TROWS, 128), f32),
        ],
        compiler_params=params(),
        name="arrange",
    )(got)


def expert_kernel(x_ref, inv_ref, w_ref, out_ref, w_vm, act_vm, sems):
    copies = []
    for f in range(8):
        copies.append(pltpu.make_async_copy(w_ref.at[f, 0:FEAT], w_vm.at[f, 0:FEAT], sems.at[f]))
    for f in range(8):
        copies.append(
            pltpu.make_async_copy(w_ref.at[f, FEAT : FEAT + 128], w_vm.at[f, FEAT : FEAT + 128], sems.at[8 + f])
        )
    for copy in copies:
        copy.start()
    for f in range(8):
        copies[f].wait()
        part = jnp.dot(x_ref[f], w_vm[f, 0:FEAT, :], preferred_element_type=f32)
        if f == 0:
            act_vm[...] = part
        else:
            act_vm[...] += part
    inv = inv_ref[:, 0:1]
    gate = act_vm[:, 0:MAIN] * inv
    up = act_vm[:, MAIN : 2 * MAIN] * inv
    main = (gate * jax.nn.sigmoid(gate) * up).astype(bf16)
    rest = act_vm[:, 2 * MAIN : WIDE] * inv
    gate_t, up_t = rest[:, 0:TAIL], rest[:, TAIL : 2 * TAIL]
    tail = (gate_t * jax.nn.sigmoid(gate_t) * up_t).astype(bf16)
    for f in range(8):
        copies[8 + f].wait()
        wd = jnp.concatenate([w_vm[f, FEAT : FEAT + 128, q * 256 : (q + 1) * 256] for q in range(MAIN // 128)], axis=0)
        wt = jnp.concatenate(
            [w_vm[f, FEAT : FEAT + TAIL, 2 * MAIN : WIDE], w_vm[f, FEAT + TAIL : FEAT + 128, 2 * MAIN : WIDE]], axis=1
        )
        res = jnp.dot(main, wd, preferred_element_type=f32) + jnp.dot(tail, wt, preferred_element_type=f32)
        for i in range(PER):
            piece = res[i * ROWS : (i + 1) * ROWS, :].reshape(8, 8, FEAT)
            out_ref[:, f * 8 : (f + 1) * 8, i * FEAT : (i + 1) * FEAT] = piece.astype(bf16)


def experts(x, inv, weights):
    vm = pl.BlockSpec(memory_space=pltpu.VMEM)
    return pl.pallas_call(
        expert_kernel,
        in_specs=[vm, vm, pl.BlockSpec(memory_space=pl.ANY)],
        out_specs=vm,
        out_shape=jax.ShapeDtypeStruct((8, ROWS, SLOTS_W), bf16),
        scratch_shapes=[
            pltpu.VMEM((8, FEAT + 128, WIDE), bf16),
            pltpu.VMEM((TROWS, WIDE), f32),
            pltpu.SemaphoreType.DMA((16,)),
        ],
        compiler_params=params(),
        name="experts",
    )(x, inv, weights)


def reduce_kernel(got_ref, out_ref):
    total = got_ref[0].astype(f32)
    for j in range(1, 8):
        total = total + got_ref[j].astype(f32)
    out_ref[...] = total.astype(bf16)


def reduce_parts(got):
    return pl.pallas_call(
        reduce_kernel,
        out_shape=jax.ShapeDtypeStruct((ROWS, SLOTS_W), bf16),
        compiler_params=params(),
        name="reduce_parts",
    )(got)


def combine_kernel(got_ref, mix_ref, ids_ref, eg_ref, out_ref):
    dest = slot_dests(ids_ref[...])
    gates = eg_ref[...]
    total = mix_ref[...]
    for k in range(2):
        picked = jnp.zeros((TOK, FEAT), f32)
        for i in range(PER):
            pick = jnp.where(dest[k] == slot_values(i), 1.0, 0.0).astype(bf16)
            picked = picked + jnp.dot(pick, got_ref[:, i * FEAT : (i + 1) * FEAT], preferred_element_type=f32)
        total = total + gates[:, k : k + 1] * picked
    out_ref[...] = total.astype(bf16)


def combine(got, mixed_in, ids, gates):
    return pl.pallas_call(
        combine_kernel,
        out_shape=jax.ShapeDtypeStruct((TOK, FEAT), bf16),
        compiler_params=params(),
        name="combine",
    )(got, mixed_in, ids, gates)


def on_device(
    queries, new_keys, new_values, cache_keys, cache_values, lengths, att_gates, resid, norm_gain,
    expert_ids, expert_gates, w_gate, w_up, w_down,
):
    packed = pack_weights(w_gate, w_up, w_down)
    weights = lax.all_gather(packed, "y")
    attended, mixed_in, send = attend(
        lengths, queries.reshape(TOK, 2 * FEAT), new_keys, new_values, cache_keys, cache_values,
        att_gates, resid, norm_gain.reshape(1, FEAT), expert_ids,
    )
    got = lax.all_to_all(send, ("y", "z"), 0, 0, tiled=True)
    got = jnp.broadcast_to(got[None], (8, ROWS, SEND_W))
    got = lax.all_to_all(got, ("x", "c"), 0, 0, tiled=True)
    x, inv = arrange(got)
    part = experts(x, inv, weights)
    part = lax.all_to_all(part, ("x", "c"), 0, 0, tiled=True)
    done = reduce_parts(part)
    done = lax.all_to_all(done, ("y", "z"), 0, 0, tiled=True)
    mixed = combine(done, mixed_in, expert_ids, expert_gates)
    return attended, mixed


def solution(mesh):
    grid = Mesh(mesh.devices.reshape(8, 4, 2, 8), ("z", "x", "c", "y"))
    dp = ("z", "x", "c")
    in_specs = (
        P(dp, None, "y"),
        P(dp, "y"),
        P(dp, "y"),
        P(dp, None, "y"),
        P(dp, None, "y"),
        P(dp),
        P(dp, None),
        P(dp, "y"),
        P("y"),
        P(dp, None),
        P(dp, None),
        P(dp, "y", None),
        P(dp, "y", None),
        P(dp, None, "y"),
    )
    out_specs = (P(dp, "y"), P(dp, "y"))
    return jax.shard_map(on_device, mesh=grid, in_specs=in_specs, out_specs=out_specs, check_vma=False)
```
